256 devices in a mesh: aa: 8 (over z), ba: 32 (over x, y, core).
Axes of the slice: x: 4, y: 4, z: 8, core: 2. Of those that a mesh axis runs over, the one named last changes fastest.
Arguments:
- deltas: bfloat16 [1048576, 128], P(('aa', 'ba')), may hold values from -6 to 6
- row_ids: int32 [1048576], P(('aa', 'ba')), may hold values from 0 to 4095, as said below
- sample_counts: int32 [1048576], P(('aa', 'ba')), may hold values from 1 to 8
- live: int32 [1048576], P(('aa', 'ba')), may hold values from 0 to 1, as said below
- table: float32 [1048576, 128], P(('aa', 'ba')), may hold values from -6 to 6
- accum: float32 [1048576, 128], P(('aa', 'ba')), may hold values from 0.01 to 1
Outputs:
- new_table: float32 [1048576, 128], P(('aa', 'ba'))
- new_accum: float32 [1048576, 128], P(('aa', 'ba'))
- fresh_rows: bfloat16 [1048576, 128], P(('aa', 'ba'))
The draws below stay inside these ranges and needn't reach their ends.
Inputs may be any that keep to these rules, and one draw needn't show every extreme that they name: `row_ids`: A replica's 4096 slots are 256 blocks of 16; block j holds rows of owner j, given as offsets among its 4096 rows, pairwise distinct within the block. In each block of 16 slots the live ones come first; every replica has some block with all 16 slots live.
All inputs are finite; a program needn't handle non-finite values.
Results may differ from the reference program's by a relative error of at most 0.0012.
Values may be sent and summed in bfloat16 or wider, within the bound.
A program may use at most 64 MiB of HBM per device.

```python
import math
import jax
import jax.numpy as jnp

WIDTH = 128
ROWS_DEV = 4096
CAP = 16
REPLICAS = 256
SLOTS = 4096
ROWS = 1048576


def slot_layout(key):
    keys = jax.random.split(jax.random.fold_in(key, 71), 5)
    heat = jax.random.randint(keys[0], (REPLICAS,), 1, 5)
    spread = jax.random.randint(keys[1], (REPLICAS, REPLICAS), 0, max(1, CAP // 4) + 1)
    filled = CAP - spread * heat[None, :] // 4
    chosen = jax.random.randint(keys[2], (REPLICAS,), 0, REPLICAS)
    owners = jnp.arange(REPLICAS, dtype=jnp.int32)
    filled = jnp.where(owners[None, :] == chosen[:, None], CAP, filled)
    within = jnp.arange(CAP, dtype=jnp.int32)
    marks = (within[None, None, :] < filled[:, :, None]).astype(jnp.int32)
    anchor = jax.random.randint(keys[3], (REPLICAS, REPLICAS, 1), 0, ROWS_DEV)
    stride = jax.random.randint(keys[4], (REPLICAS, REPLICAS, 1), 0, ROWS_DEV // 2) * 2 + 1
    offset = (anchor + within[None, None, :] * stride) % ROWS_DEV
    return (offset.reshape(-1).astype(jnp.int32), marks.reshape(-1))


def draw_row_ids(key, part):
    return slot_layout(key)[0]


def draw_live(key, part):
    return slot_layout(key)[1]


def place_ends(array, own_key, least, largest):
    index_at = [jax.random.randint(jax.random.fold_in(own_key, axis), (), 0, length) for axis, length in enumerate(array.shape)]
    widest = array.shape.index(max(array.shape))
    next_to = index_at[:widest] + [(index_at[widest] + 1) % array.shape[widest]] + index_at[widest + 1:]
    return array.at[tuple(index_at)].set(least).at[tuple(next_to)].set(largest)


def steps_of(own_key, extent, cuts, least, top_value):
    loudness, own = 1.0, jax.random.fold_in(own_key, 6)
    for dim, parts in cuts:
        heights = jnp.exp(jax.random.uniform(jax.random.fold_in(own, dim), (parts,), jnp.float32, least / len(cuts), top_value / len(cuts)))
        loudness = loudness * jnp.repeat(heights, extent[dim] // parts).reshape([-1 if axis == dim else 1 for axis in range(len(extent))])
    return loudness


def scatter_about(stream_key, extent, scale, reach, cuts=(), held_as=jnp.bfloat16):
    entries = scale * jax.random.normal(stream_key, extent, jnp.float32)
    if cuts:
        entries = entries * steps_of(stream_key, extent, cuts, -0.22, 0.18)
    return jnp.clip(entries, -reach, reach).astype(held_as)


def setup_inputs(seed: int = 0) -> dict:
    splits = jax.random.split(jax.random.key(seed), 7)
    return {
        "deltas": scatter_about(splits[0], (REPLICAS * SLOTS, WIDTH), 1.0, 6.0, ((0, 256),)),
        "row_ids": draw_row_ids(jax.random.fold_in(splits[6], 71), 0),
        "sample_counts": place_ends(jax.random.randint(splits[2], (REPLICAS * SLOTS,), 1, 9), jax.random.fold_in(splits[2], 1), 1, 8).astype(jnp.int32),
        "live": draw_live(jax.random.fold_in(splits[6], 71), 0),
        "table": scatter_about(splits[4], (ROWS, WIDTH), 1.0, 6.0, ((0, 256),), jnp.float32),
        "accum": jnp.clip(jnp.exp(math.log(1.0) - 4.6051702 * jax.random.uniform(splits[5], (ROWS, WIDTH), jnp.float32) ** steps_of(splits[5], (ROWS, WIDTH), ((0, 256),), -0.2, 0.2)), 0.01, 1.0),
    }


learn_rate = 0.1
epsilon = 1e-08

def reference(deltas, row_ids, sample_counts, live, table, accum):
    count = row_ids.shape[0]
    position = jnp.arange(count, dtype=jnp.int32)
    row = (position // CAP % REPLICAS).astype(jnp.int32) * ROWS_DEV + row_ids.astype(jnp.int32)
    weight = (sample_counts * live).astype(jnp.float32)
    terms = deltas.astype(jnp.float32) * weight[:, None]
    numer = jax.ops.segment_sum(terms, row, num_segments=table.shape[0])
    total = jax.ops.segment_sum(weight, row, num_segments=table.shape[0])
    grad = numer / jnp.maximum(total, 1.0)[:, None]
    new_accum = accum + grad * grad
    new_table = table - learn_rate * grad / (jnp.sqrt(new_accum) + epsilon)
    fresh_rows = new_table[row].astype(jnp.bfloat16)
    return (new_table, new_accum, fresh_rows)
```

```python
import jax
import jax.numpy as jnp
from jax import lax
from jax.experimental import pallas as pl
from jax.experimental.pallas import tpu as pltpu
from jax.sharding import PartitionSpec as P

learn_rate = 0.1
epsilon = 1e-08
MESH = pl.DeviceIdType.MESH
DMA = pltpu.SemaphoreType.DMA


def offset(p):
    return (p + 1) // 2 * (2 * (p % 2) - 1)


def partner(b, k):
    core, y, x = b % 2, b // 2 % 4, b // 8
    return ((x + k // 8) % 4 * 4 + (y + k // 2 % 4) % 4) * 2 + (core + k % 2) % 2


def landed(ref, sem):
    pltpu.make_async_copy(ref, ref, sem).wait()


def send(src, dst, send_sem, recv_sem, a, b):
    pltpu.make_async_remote_copy(
        src, dst, send_sem, recv_sem, device_id=(a, b), device_id_type=MESH
    ).start()


def swap_blocks(m):
    row = lax.broadcasted_iota(jnp.int32, m.shape, 0)
    block = lax.broadcasted_iota(jnp.int32, m.shape, 1) // 16
    out = jnp.zeros_like(m)
    for d in range(8):
        t = m if d == 0 else pltpu.roll(pltpu.roll(m, 8 - d, 0), 16 * d, 1)
        out = jnp.where(block == (row + d) % 8, t, out)
    return out


def kernel(
    deltas, ids, counts, live, table, accum,
    new_table, new_accum, fresh,
    tab, acc, numer, upper, zbuf, got, rep, rbuf, id_src, id_mid, id_row, id_got, id_lane, id_col,
    tab_sem, acc_sem, tab_out, acc_out, own_sem, back_sem,
    id_zsend, id_zrecv, id_bsend, id_brecv,
    zsend, zrecv, bsend, brecv, rzsend, rzrecv, rbsend, rbrecv,
):
    a, b = lax.axis_index("aa"), lax.axis_index("ba")
    rows = tab.shape[0]
    load_tab = pltpu.make_async_copy(table, tab, tab_sem)
    load_acc = pltpu.make_async_copy(accum, acc, acc_sem)
    load_tab.start()
    load_acc.start()

    barrier = pltpu.get_barrier_semaphore()
    for d in range(1, 8):
        pl.semaphore_signal(barrier, inc=1, device_id=((a + d) % 8, b), device_id_type=MESH)

    def greet(k, _):
        pl.semaphore_signal(barrier, inc=1, device_id=(a, partner(b, k)), device_id_type=MESH)
        return 0

    lax.fori_loop(1, 32, greet, 0)
    packed = ids[...] + counts[...] * live[...] * 65536
    for i in range(8):
        id_src[i] = packed[4 * i : 4 * i + 4]
    pl.semaphore_wait(barrier, 38)

    def ids_along(p, _):
        pa = (a + offset(p) + 8) % 8
        send(id_src.at[pa], id_mid.at[p], id_zsend, id_zrecv, pa, b)
        return 0

    lax.fori_loop(1, 8, ids_along, 0)

    def deltas_along(p, _):
        pa = (a + offset(p) + 8) % 8
        send(deltas.at[pl.ds(32 * pa, 32)], zbuf.at[p - 1], zsend, zrecv.at[p], pa, b)
        return 0

    lax.fori_loop(1, 8, deltas_along, 0)
    id_mid[0] = id_src[a]

    def spread(src, p):
        pltpu.make_async_copy(src.at[b], got.at[32 * p + b], own_sem.at[p]).start()

        def one(k, _):
            pb = partner(b, k)
            send(src.at[pb], got.at[32 * p + b], bsend, brecv.at[p], a, pb)
            return 0

        lax.fori_loop(1, 32, one, 0)

    spread(deltas.at[pl.ds(32 * a, 32)], 0)
    landed(id_mid.at[pl.ds(1, 7)], id_zrecv)
    for r in range(4):
        id_row[8 * r : 8 * r + 8, 0, :] = swap_blocks(id_mid[:, r, :])

    def ids_across(k, _):
        pb = partner(b, k)
        send(id_row.at[pb], id_got.at[b], id_bsend, id_brecv, a, pb)
        return 0

    lax.fori_loop(1, 32, ids_across, 0)
    id_got[b] = id_row[b]
    numer[...] = jnp.zeros_like(numer)

    landed(zbuf.at[0], zrecv.at[1])
    spread(zbuf.at[0], 1)
    landed(id_got.at[pl.ds(0, 31)], id_brecv)
    for r in range(4):
        id_lane[:, 128 * r : 128 * r + 128] = swap_blocks(id_got[8 * r : 8 * r + 8, 0, :])

    def scatter(p):
        landed(got.at[pl.ds(0, 31)], brecv.at[p])
        landed(got.at[0], own_sem.at[p])
        both = id_lane[pl.ds(p, 1), :]
        row = both % 65536
        weight = (both // 65536).astype(jnp.float32)
        values = got[pl.ds(32 * p, 32)].reshape(512, 128)
        values = jnp.concatenate([values, jnp.ones_like(values)], axis=1)

        def block(i, _):
            base = pl.multiple_of(i * 256, 256)
            here = lax.broadcasted_iota(jnp.int32, (256, 512), 0) == row - base
            picks = jnp.where(here, weight, 0.0).astype(jnp.bfloat16)
            numer[pl.ds(base, 256), :] += jnp.dot(
                picks, values, preferred_element_type=jnp.float32
            )
            return 0

        lax.fori_loop(0, rows // 256, block, 0)

    def incoming(p, _):
        landed(zbuf.at[p - 1], zrecv.at[p])
        spread(zbuf.at[p - 1], p)
        scatter(p - 2)
        return 0

    lax.fori_loop(2, 8, incoming, 0)
    scatter(6)
    scatter(7)

    load_tab.wait()
    load_acc.wait()

    def update(i, _):
        at = pl.ds(pl.multiple_of(i * 256, 256), 256)
        grad = numer[at, 0:128] / jnp.maximum(numer[at, 128:256], 1.0)
        accum_next = acc[at, :] + grad * grad
        table_next = tab[at, :] - learn_rate * grad / (jnp.sqrt(accum_next) + epsilon)
        acc[at, :] = accum_next
        tab[at, :] = table_next
        upper[at, :] = table_next.astype(jnp.bfloat16)
        return 0

    lax.fori_loop(0, rows // 256, update, 0)
    store_tab = pltpu.make_async_copy(tab, new_table, tab_out)
    store_acc = pltpu.make_async_copy(acc, new_accum, acc_out)
    store_tab.start()
    store_acc.start()

    def gather(p):
        row = id_lane[pl.ds(p, 1), :] % 65536
        id_col[...] = jnp.broadcast_to(row, (128, 512)).T
        total = jnp.zeros((512, 128), jnp.float32)
        lane = lax.broadcasted_iota(jnp.int32, (512, 128), 1)
        column = id_col[...] - lane
        for k in range(rows // 256):
            picks = jnp.concatenate(
                [
                    jnp.where(column == 256 * k, 1.0, 0.0).astype(jnp.bfloat16),
                    jnp.where(column == 256 * k + 128, 1.0, 0.0).astype(jnp.bfloat16),
                ],
                axis=1,
            )
            total += jnp.dot(picks, upper[256 * k : 256 * k + 256, :], preferred_element_type=jnp.float32)
        rep[pl.ds(32 * p, 32)] = total.astype(jnp.bfloat16).reshape(32, 16, 128)

    def reply(p):
        gather(p)
        pa = (a - offset(p) + 8) % 8
        send(rep.at[pl.ds(32 * p, 32)], rbuf.at[p - 1], rzsend, rzrecv.at[p], pa, b)

    def deliver(src, p):
        owner = (a + offset(p) + 8) % 8
        pltpu.make_async_copy(src.at[b], fresh.at[32 * owner + b], back_sem).start()

        def one(k, _):
            pb = partner(b, k)
            send(src.at[pb], fresh.at[32 * owner + b], rbsend, rbrecv, a, pb)
            return 0

        lax.fori_loop(1, 32, one, 0)

    def first(i, _):
        reply(7 - i)
        return 0

    def later(i, _):
        reply(7 - i)
        p = 10 - i
        landed(rbuf.at[p - 1], rzrecv.at[p])
        deliver(rbuf.at[p - 1], p)
        return 0

    lax.fori_loop(0, 3, first, 0)
    lax.fori_loop(3, 7, later, 0)
    gather(0)
    deliver(rep.at[pl.ds(0, 32)], 0)

    def last(i, _):
        p = 3 - i
        landed(rbuf.at[p - 1], rzrecv.at[p])
        deliver(rbuf.at[p - 1], p)
        return 0

    lax.fori_loop(0, 3, last, 0)

    landed(id_src.at[pl.ds(0, 7)], id_zsend)
    landed(id_row.at[pl.ds(0, 31)], id_bsend)
    landed(zbuf, zsend)
    landed(rbuf, rzsend)
    landed(fresh.at[pl.ds(0, 8)], back_sem)
    for sem, ref in ((bsend, got), (rbsend, got), (rbrecv, fresh)):
        landed(ref.at[pl.ds(0, 248)], sem)
    store_tab.wait()
    store_acc.wait()


def on_device(deltas, row_ids, sample_counts, live, table, accum):
    rows, width = table.shape
    blocks = (256, 16, width)
    small = (32, 128)
    anywhere = pl.BlockSpec(memory_space=pl.ANY)
    vmem = pl.BlockSpec(memory_space=pltpu.VMEM)
    bf16, f32, i32 = jnp.bfloat16, jnp.float32, jnp.int32
    V = pltpu.VMEM
    new_table, new_accum, fresh = pl.pallas_call(
        kernel,
        name="exchange",
        out_shape=(
            jax.ShapeDtypeStruct((rows, width), f32),
            jax.ShapeDtypeStruct((rows, width), f32),
            jax.ShapeDtypeStruct(blocks, bf16),
        ),
        in_specs=[anywhere, vmem, vmem, vmem, anywhere, anywhere],
        out_specs=(anywhere, anywhere, anywhere),
        scratch_shapes=[
            V((rows, width), f32), V((rows, width), f32), V((rows, 2 * width), f32), V((rows, width), bf16),
            V((7, 32, 16, width), bf16), V(blocks, bf16), V(blocks, bf16), V((7, 32, 16, width), bf16),
            V((8, 4, 128), i32), V((8, 4, 128), i32), V((32, 1, 128), i32), V((32, 1, 128), i32),
            V((8, 512), i32), V((512, 128), i32),
            DMA, DMA, DMA, DMA, DMA((8,)), DMA,
            DMA, DMA, DMA, DMA,
            DMA, DMA((8,)), DMA, DMA((8,)), DMA, DMA((8,)), DMA, DMA,
        ],
        compiler_params=pltpu.CompilerParams(
            collective_id=1, has_side_effects=True, vmem_limit_bytes=48 << 20
        ),
    )(
        deltas.reshape(blocks), row_ids.reshape(small), sample_counts.reshape(small),
        live.reshape(small), table, accum,
    )
    return new_table, new_accum, fresh.reshape(-1, width)


def solution(mesh):
    rows, slots = P(("aa", "ba"), None), P(("aa", "ba"))
    return jax.shard_map(
        on_device,
        mesh=mesh,
        in_specs=(rows, slots, slots, slots, rows, rows),
        out_specs=(rows, rows, rows),
        check_vma=False,
    )
```

```python
import jax
import jax.numpy as jnp
from jax import lax
from jax.experimental import pallas as pl
from jax.experimental.pallas import tpu as pltpu
from jax.sharding import PartitionSpec as P

learn_rate = 0.1
epsilon = 1e-08
MESH = pl.DeviceIdType.MESH
DMA = pltpu.SemaphoreType.DMA


def offset(p):
    return (p + 1) // 2 * (2 * (p % 2) - 1)


def partner(b, k):
    core, y, x = b % 2, b // 2 % 4, b // 8
    return ((x + k // 8) % 4 * 4 + (y + k // 2 % 4) % 4) * 2 + (core + k % 2) % 2


def partner_back(b, k):
    core, y, x = b % 2, b // 2 % 4, b // 8
    return ((x + 4 - k // 8) % 4 * 4 + (y + 4 - k // 2 % 4) % 4) * 2 + (core + k % 2) % 2


def landed(ref, sem):
    pltpu.make_async_copy(ref, ref, sem).wait()


def send(src, dst, send_sem, recv_sem, a, b):
    pltpu.make_async_remote_copy(
        src, dst, send_sem, recv_sem, device_id=(a, b), device_id_type=MESH
    ).start()


def swap_blocks(m):
    row = lax.broadcasted_iota(jnp.int32, m.shape, 0)
    block = lax.broadcasted_iota(jnp.int32, m.shape, 1) // 16
    out = jnp.zeros_like(m)
    for d in range(8):
        t = m if d == 0 else pltpu.roll(pltpu.roll(m, 8 - d, 0), 16 * d, 1)
        out = jnp.where(block == (row + d) % 8, t, out)
    return out


def kernel(
    deltas, ids, counts, live, table, accum,
    new_table, new_accum, fresh,
    src, tab, acc, numer, upper, got, rep, ints, id_src, id_mid, id_row, id_got, lows,
    in_sem, tab_sem, acc_sem, int_sem, tab_out, acc_out, own_sem, ready,
    id_zsend, id_zrecv, id_bsend, id_brecv, dsend, drecv, rsend, rrecv,
):
    a, b = lax.axis_index("aa"), lax.axis_index("ba")
    me = 32 * a + b
    rows = tab.shape[0]
    load_ints = [
        pltpu.make_async_copy(x, ints.at[i], int_sem.at[i]) for i, x in enumerate((ids, counts, live))
    ]
    load_src = pltpu.make_async_copy(deltas, src, in_sem)
    load_tab = pltpu.make_async_copy(table, tab, tab_sem)
    load_acc = pltpu.make_async_copy(accum, acc, acc_sem)
    for copy in (*load_ints, load_src, load_tab, load_acc):
        copy.start()

    barrier = pltpu.get_barrier_semaphore()
    for d in range(1, 8):
        pl.semaphore_signal(barrier, inc=1, device_id=((a + d) % 8, b), device_id_type=MESH)

    def greet(k, _):
        pl.semaphore_signal(barrier, inc=1, device_id=(a, partner(b, k)), device_id_type=MESH)
        return 0

    lax.fori_loop(1, 32, greet, 0)
    for copy in load_ints:
        copy.wait()
    packed = ints[0] + ints[1] * ints[2] * 65536
    for i in range(8):
        id_src[i] = packed[4 * i : 4 * i + 4]
    load_src.wait()
    pl.semaphore_wait(barrier, 38)
    for d in range(1, 8):
        pl.semaphore_signal(ready, inc=1, device_id=((a + d) % 8, b), device_id_type=MESH)

    def ids_along(p, _):
        pa = (a + offset(p) + 8) % 8
        send(id_src.at[pa], id_mid.at[p], id_zsend, id_zrecv, pa, b)
        return 0

    lax.fori_loop(1, 8, ids_along, 0)
    id_mid[0] = id_src[a]

    def deltas_to(k, p):
        pa, pb = (a + offset(p) + 8) % 8, partner(b, k)
        send(src.at[32 * pa + pb], got.at[8 * k + p], dsend, drecv.at[k // 4], pa, pb)

    def plane_near(p, _):
        deltas_to(0, p)
        return 0

    own = pltpu.make_async_copy(src.at[me], got.at[0], own_sem)
    own.start()
    lax.fori_loop(1, 8, plane_near, 0)
    pl.semaphore_wait(ready, 7)

    def plane(k, _):
        for p in (1, 2, 3, 4, 5, 6, 7, 0):
            deltas_to(k, p)
        return 0

    lax.fori_loop(1, 4, plane, 0)
    landed(id_mid.at[pl.ds(1, 7)], id_zrecv)
    for r in range(4):
        id_row[8 * r : 8 * r + 8, 0, :] = swap_blocks(id_mid[:, r, :])

    def ids_across(k, _):
        pb = partner(b, k)
        send(id_row.at[pb], id_got.at[k], id_bsend, id_brecv, a, pb)
        return 0

    lax.fori_loop(1, 32, ids_across, 0)
    id_got[0] = id_row[b]
    lax.fori_loop(4, 32, plane, 0)
    numer[...] = jnp.zeros_like(numer)
    landed(id_got.at[pl.ds(0, 31)], id_brecv)

    def scatter(g, count):
        landed(got.at[pl.ds(0, count)], drecv.at[g])
        lanes = [id_got[4 * g + i] for i in range(4)]
        both = jnp.concatenate(lanes, axis=1)
        row = both % 65536
        high = row // 256
        weight = (both // 65536).astype(jnp.float32)
        low = lax.broadcasted_iota(jnp.int32, (256, 512), 0) == row % 256
        lows[...] = jnp.where(low, 1.0, 0.0).astype(jnp.bfloat16)
        values = got[pl.ds(32 * g, 32)].reshape(512, 128)
        values = jnp.concatenate([values, jnp.ones_like(values)], axis=1)

        def block(i, _):
            base = pl.multiple_of(i * STEP, STEP)
            picks = []
            for j in range(STEP // 256):
                w = jnp.where(high == i * (STEP // 256) + j, weight, 0.0)
                w = jnp.broadcast_to(w, (16, 512)).astype(jnp.bfloat16)
                w = jnp.concatenate([w] * 16, axis=0)
                picks.append(lows[...] * w)
            numer[pl.ds(base, STEP), :] += jnp.dot(
                jnp.concatenate(picks, axis=0), values, preferred_element_type=jnp.float32
            )
            return 0

        lax.fori_loop(0, rows // STEP, block, 0)

    own.wait()
    scatter(0, 31)

    def incoming(g, _):
        scatter(g, 32)
        return 0

    lax.fori_loop(1, 8, incoming, 0)

    load_tab.wait()
    load_acc.wait()

    def update(i, _):
        at = pl.ds(pl.multiple_of(i * 256, 256), 256)
        grad = numer[at, 0:128] / jnp.maximum(numer[at, 128:256], 1.0)
        accum_next = acc[at, :] + grad * grad
        table_next = tab[at, :] - learn_rate * grad / (jnp.sqrt(accum_next) + epsilon)
        acc[at, :] = accum_next
        tab[at, :] = table_next
        upper[at, :] = table_next.astype(jnp.bfloat16)
        return 0

    lax.fori_loop(0, rows // 256, update, 0)
    store_tab = pltpu.make_async_copy(tab, new_table, tab_out)
    store_acc = pltpu.make_async_copy(acc, new_accum, acc_out)

    def gather(g):
        columns = [jnp.broadcast_to(id_got[4 * g + i] % 65536, (128, 128)).T for i in range(4)]
        row = jnp.concatenate(columns, axis=0)
        high = (row // 256).astype(jnp.float32).astype(jnp.bfloat16)
        lane = lax.broadcasted_iota(jnp.int32, (512, 128), 1)
        row = row % 256
        near = jnp.where(row == lane, 1.0, 0.0).astype(jnp.bfloat16)
        far = jnp.where(row == lane + 128, 1.0, 0.0).astype(jnp.bfloat16)
        low = jnp.concatenate([near, far], axis=1)
        high = jnp.concatenate([high, high], axis=1)
        zero = jnp.zeros_like(low)
        picks = jnp.concatenate(
            [jnp.where(high == float(k), low, zero) for k in range(rows // 256)], axis=1
        )
        total = jnp.dot(picks, upper[...], preferred_element_type=jnp.float32)
        rep[pl.ds(32 * g, 32)] = total.astype(jnp.bfloat16).reshape(32, 16, 128)

    def reply(k, p):
        pa, pb = (a - offset(p) + 8) % 8, partner_back(b, k)
        send(rep.at[8 * k + p], fresh.at[me], rsend, rrecv, pa, pb)

    def replies(k, _):
        for p in (1, 2, 3, 4, 5, 6, 7, 0):
            reply(k, p)
        return 0

    gather(0)
    back = pltpu.make_async_copy(rep.at[0], fresh.at[me], own_sem)
    back.start()
    for p in range(1, 8):
        reply(0, p)
    lax.fori_loop(1, 4, replies, 0)
    store_tab.start()
    store_acc.start()

    def outgoing(g, _):
        gather(g)
        lax.fori_loop(4 * g, 4 * g + 4, replies, 0)
        return 0

    lax.fori_loop(1, 8, outgoing, 0)

    landed(id_src.at[pl.ds(0, 7)], id_zsend)
    landed(id_row.at[pl.ds(0, 31)], id_bsend)
    back.wait()
    landed(got.at[pl.ds(0, 255)], dsend)
    landed(rep.at[pl.ds(0, 255)], rsend)
    landed(fresh.at[pl.ds(0, 255)], rrecv)
    store_tab.wait()
    store_acc.wait()


STEP = 1024


def on_device(deltas, row_ids, sample_counts, live, table, accum):
    rows, width = table.shape
    blocks = (256, 16, width)
    small = (32, 128)
    anywhere = pl.BlockSpec(memory_space=pl.ANY)
    hbm = pl.BlockSpec(memory_space=pltpu.HBM)
    bf16, f32, i32 = jnp.bfloat16, jnp.float32, jnp.int32
    V = pltpu.VMEM
    new_table, new_accum, fresh = pl.pallas_call(
        kernel,
        name="exchange",
        out_shape=(
            jax.ShapeDtypeStruct((rows, width), f32),
            jax.ShapeDtypeStruct((rows, width), f32),
            jax.ShapeDtypeStruct(blocks, bf16),
        ),
        in_specs=[hbm] * 6,
        out_specs=(anywhere, anywhere, anywhere),
        scratch_shapes=[
            V(blocks, bf16), V((rows, width), f32), V((rows, width), f32), V((rows, 2 * width), f32),
            V((rows, width), bf16), V(blocks, bf16), V(blocks, bf16), V((3, 32, 128), i32),
            V((8, 4, 128), i32), V((8, 4, 128), i32), V((32, 1, 128), i32), V((32, 1, 128), i32),
            V((256, 512), bf16),
            DMA, DMA, DMA, DMA((3,)), DMA, DMA, DMA, pltpu.SemaphoreType.REGULAR,
            DMA, DMA, DMA, DMA, DMA, DMA((8,)), DMA, DMA,
        ],
        compiler_params=pltpu.CompilerParams(
            collective_id=1, has_side_effects=True, vmem_limit_bytes=48 << 20
        ),
    )(
        deltas.reshape(blocks), row_ids.reshape(small), sample_counts.reshape(small),
        live.reshape(small), table, accum,
    )
    return new_table, new_accum, fresh.reshape(-1, width)


def solution(mesh):
    rows, slots = P(("aa", "ba"), None), P(("aa", "ba"))
    return jax.shard_map(
        on_device,
        mesh=mesh,
        in_specs=(rows, slots, slots, slots, rows, rows),
        out_specs=(rows, rows, rows),
        check_vma=False,
    )
```

```python
import jax
import jax.numpy as jnp
from jax import lax
from jax.experimental import pallas as pl
from jax.experimental.pallas import tpu as pltpu
from jax.sharding import PartitionSpec as P

learn_rate = 0.1
epsilon = 1e-08
MESH = pl.DeviceIdType.MESH
DMA = pltpu.SemaphoreType.DMA


def offset(p):
    return (p + 1) // 2 * (2 * (p % 2) - 1)


def partner(b, k):
    core, y, x = b % 2, b // 2 % 4, b // 8
    return ((x + k // 8) % 4 * 4 + (y + k // 2 % 4) % 4) * 2 + (core + k % 2) % 2


def partner_back(b, k):
    core, y, x = b % 2, b // 2 % 4, b // 8
    return ((x + 4 - k // 8) % 4 * 4 + (y + 4 - k // 2 % 4) % 4) * 2 + (core + k % 2) % 2


def landed(ref, sem):
    pltpu.make_async_copy(ref, ref, sem).wait()


def send(src, dst, send_sem, recv_sem, a, b):
    pltpu.make_async_remote_copy(
        src, dst, send_sem, recv_sem, device_id=(a, b), device_id_type=MESH
    ).start()


def swap_blocks(m):
    row = lax.broadcasted_iota(jnp.int32, m.shape, 0)
    block = lax.broadcasted_iota(jnp.int32, m.shape, 1) // 16
    out = jnp.zeros_like(m)
    for d in range(8):
        t = m if d == 0 else pltpu.roll(pltpu.roll(m, 8 - d, 0), 16 * d, 1)
        out = jnp.where(block == (row + d) % 8, t, out)
    return out


def kernel(
    deltas, ids, counts, live, table, accum,
    tab, acc, fresh,
    src, numer, upper, got, rep, ints, id_src, id_mid, id_row, id_got, lows,
    in_sem, tab_sem, acc_sem, int_sem, own_sem, ready,
    id_zsend, id_zrecv, id_bsend, id_brecv, dsend, drecv, rsend, rrecv,
):
    a, b = lax.axis_index("aa"), lax.axis_index("ba")
    me = 32 * a + b
    rows = tab.shape[0]
    load_ints = [
        pltpu.make_async_copy(x, ints.at[i], int_sem.at[i]) for i, x in enumerate((ids, counts, live))
    ]
    load_src = pltpu.make_async_copy(deltas, src, in_sem)
    load_tab = pltpu.make_async_copy(table, tab, tab_sem)
    load_acc = pltpu.make_async_copy(accum, acc, acc_sem)
    for copy in (*load_ints, load_src, load_tab, load_acc):
        copy.start()

    barrier = pltpu.get_barrier_semaphore()
    for d in range(1, 8):
        pl.semaphore_signal(barrier, inc=1, device_id=((a + d) % 8, b), device_id_type=MESH)

    def greet(k, _):
        pl.semaphore_signal(barrier, inc=1, device_id=(a, partner(b, k)), device_id_type=MESH)
        return 0

    lax.fori_loop(1, 32, greet, 0)
    for copy in load_ints:
        copy.wait()
    packed = ints[0] + ints[1] * ints[2] * 65536
    for i in range(8):
        id_src[i] = packed[4 * i : 4 * i + 4]
    load_src.wait()
    pl.semaphore_wait(barrier, 38)
    for d in range(1, 8):
        pl.semaphore_signal(ready, inc=1, device_id=((a + d) % 8, b), device_id_type=MESH)

    def ids_along(p, _):
        pa = (a + offset(p) + 8) % 8
        send(id_src.at[pa], id_mid.at[p], id_zsend, id_zrecv, pa, b)
        return 0

    lax.fori_loop(1, 8, ids_along, 0)
    id_mid[0] = id_src[a]

    def deltas_to(k, p):
        group = k // 4 + k // 30
        pa, pb = (a + offset(p) + 8) % 8, partner(b, k)
        send(src.at[32 * pa + pb], got.at[8 * k + p], dsend, drecv.at[group], pa, pb)

    def plane_near(p, _):
        deltas_to(0, p)
        return 0

    own = pltpu.make_async_copy(src.at[me], got.at[0], own_sem)
    own.start()
    lax.fori_loop(1, 8, plane_near, 0)
    pl.semaphore_wait(ready, 7)

    def plane(k, _):
        for p in (7, 5, 6, 3, 4, 1, 2, 0):
            deltas_to(k, p)
        return 0

    lax.fori_loop(1, 10, plane, 0)
    landed(id_mid.at[pl.ds(1, 7)], id_zrecv)
    for r in range(4):
        id_row[8 * r : 8 * r + 8, 0, :] = swap_blocks(id_mid[:, r, :])

    def ids_across(k, _):
        pb = partner(b, k)
        send(id_row.at[pb], id_got.at[k], id_bsend, id_brecv, a, pb)
        return 0

    lax.fori_loop(1, 32, ids_across, 0)
    id_got[0] = id_row[b]
    lax.fori_loop(10, 32, plane, 0)
    numer[...] = jnp.zeros_like(numer)
    landed(id_got.at[pl.ds(0, 31)], id_brecv)

    def arrived(k, n, count, group):
        landed(got.at[pl.ds(0, count)], drecv.at[group])
        width = 128 * n
        both = jnp.concatenate([id_got[k + i] for i in range(n)], axis=1)
        row = both % 65536
        weight = (both // 65536).astype(jnp.float32)
        low = lax.broadcasted_iota(jnp.int32, (256, width), 0) == row % 256
        lows[:, 0:width] = jnp.where(low, 1.0, 0.0).astype(jnp.bfloat16)
        values = got[pl.ds(8 * k, 8 * n)].reshape(width, 128)
        return row // 256, weight, jnp.concatenate([values, jnp.ones_like(values)], axis=1)

    def partial(high, weight, values, i):
        width = values.shape[0]
        picks = []
        for j in range(STEP // 256):
            w = jnp.where(high == i * (STEP // 256) + j, weight, 0.0)
            w = jnp.broadcast_to(w, (16, width)).astype(jnp.bfloat16)
            picks.append(lows[:, 0:width] * jnp.concatenate([w] * 16, axis=0))
        return jnp.dot(jnp.concatenate(picks, axis=0), values, preferred_element_type=jnp.float32)

    def scatter(k, n, count, group):
        slots = arrived(k, n, count, group)

        def block(i, _):
            numer[pl.ds(pl.multiple_of(i * STEP, STEP), STEP), :] += partial(*slots, i)
            return 0

        lax.fori_loop(0, rows // STEP, block, 0)

    own.wait()
    scatter(0, 4, 31, 0)

    def incoming(g, _):
        scatter(4 * g, 4, 32, g)
        return 0

    lax.fori_loop(1, 7, incoming, 0)
    scatter(28, 2, 16, 7)
    load_tab.wait()
    load_acc.wait()
    last = arrived(30, 2, 16, 8)

    def update(i, _):
        at = pl.ds(pl.multiple_of(i * STEP, STEP), STEP)
        sums = numer[at, :] + partial(*last, i)
        grad = sums[:, 0:128] / jnp.maximum(sums[:, 128:256], 1.0)
        accum_next = acc[at, :] + grad * grad
        table_next = tab[at, :] - learn_rate * grad / (jnp.sqrt(accum_next) + epsilon)
        acc[at, :] = accum_next
        tab[at, :] = table_next
        upper[at, :] = table_next.astype(jnp.bfloat16)
        return 0

    lax.fori_loop(0, rows // STEP, update, 0)

    def gather(k, n):
        columns = [jnp.broadcast_to(id_got[k + i] % 65536, (128, 128)).T for i in range(n)]
        row = jnp.concatenate(columns, axis=0)
        high = (row // 256).astype(jnp.float32).astype(jnp.bfloat16)
        lane = lax.broadcasted_iota(jnp.int32, row.shape, 1)
        row = row % 256
        near = jnp.where(row == lane, 1.0, 0.0).astype(jnp.bfloat16)
        far = jnp.where(row == lane + 128, 1.0, 0.0).astype(jnp.bfloat16)
        low = jnp.concatenate([near, far], axis=1)
        high = jnp.concatenate([high, high], axis=1)
        zero = jnp.zeros_like(low)
        picks = jnp.concatenate(
            [jnp.where(high == float(k), low, zero) for k in range(rows // 256)], axis=1
        )
        total = jnp.dot(picks, upper[...], preferred_element_type=jnp.float32)
        rep[pl.ds(8 * k, 8 * n)] = total.astype(jnp.bfloat16).reshape(8 * n, 16, 128)

    def reply(k, p):
        pa, pb = (a - offset(p) + 8) % 8, partner_back(b, k)
        send(rep.at[8 * k + p], fresh.at[me], rsend, rrecv, pa, pb)

    def replies(k, _):
        for p in (7, 5, 6, 3, 4, 1, 2, 0):
            reply(k, p)
        return 0

    gather(0, 1)
    for p in range(7, 0, -1):
        reply(0, p)
    back = pltpu.make_async_copy(rep.at[0], fresh.at[me], own_sem)
    back.start()
    gather(1, 3)
    lax.fori_loop(1, 4, replies, 0)

    def outgoing(g, _):
        gather(4 * g, 4)
        lax.fori_loop(4 * g, 4 * g + 4, replies, 0)
        return 0

    lax.fori_loop(1, 8, outgoing, 0)

    landed(id_src.at[pl.ds(0, 7)], id_zsend)
    landed(id_row.at[pl.ds(0, 31)], id_bsend)
    back.wait()
    landed(got.at[pl.ds(0, 255)], dsend)
    landed(rep.at[pl.ds(0, 255)], rsend)
    landed(fresh.at[pl.ds(0, 255)], rrecv)


STEP = 1024
LIMIT = 46


def write_out(a, b, c, a_out, b_out, c_out, *sems):
    copies = [
        pltpu.make_async_copy(x, y, sem) for x, y, sem in zip((a, b, c), (a_out, b_out, c_out), sems)
    ]
    for copy in copies:
        copy.start()
    for copy in copies:
        copy.wait()


def on_device(deltas, row_ids, sample_counts, live, table, accum):
    rows, width = table.shape
    blocks = (256, 16, width)
    small = (32, 128)
    vmem = pl.BlockSpec(memory_space=pltpu.VMEM)
    hbm = pl.BlockSpec(memory_space=pltpu.HBM)
    bf16, f32, i32 = jnp.bfloat16, jnp.float32, jnp.int32
    V = pltpu.VMEM
    new_table, new_accum, fresh = pl.pallas_call(
        kernel,
        name="exchange",
        out_shape=(
            jax.ShapeDtypeStruct((rows, width), f32),
            jax.ShapeDtypeStruct((rows, width), f32),
            jax.ShapeDtypeStruct(blocks, bf16),
        ),
        in_specs=[hbm] * 6,
        out_specs=(vmem, vmem, vmem),
        scratch_shapes=[
            V(blocks, bf16), V((rows, 2 * width), f32),
            V((rows, width), bf16), V(blocks, bf16), V(blocks, bf16), V((3, 32, 128), i32),
            V((8, 4, 128), i32), V((8, 4, 128), i32), V((32, 1, 128), i32), V((32, 1, 128), i32),
            V((256, 512), bf16),
            DMA, DMA, DMA, DMA((3,)), DMA, pltpu.SemaphoreType.REGULAR,
            DMA, DMA, DMA, DMA, DMA, DMA((9,)), DMA, DMA,
        ],
        compiler_params=pltpu.CompilerParams(
            collective_id=1, has_side_effects=True, vmem_limit_bytes=LIMIT << 20
        ),
    )(
        *(pltpu.with_memory_space_constraint(x, pltpu.HBM) for x in (
        deltas.reshape(blocks), row_ids.reshape(small), sample_counts.reshape(small),
        live.reshape(small), table, accum)),
    )
    new_table, new_accum, fresh = pl.pallas_call(
        write_out,
        name="write_out",
        out_shape=(
            jax.ShapeDtypeStruct((rows, width), f32),
            jax.ShapeDtypeStruct((rows, width), f32),
            jax.ShapeDtypeStruct(blocks, bf16),
        ),
        in_specs=[vmem] * 3,
        out_specs=(hbm, hbm, hbm),
        scratch_shapes=[DMA, DMA, DMA],
        compiler_params=pltpu.CompilerParams(vmem_limit_bytes=2 << 20),
    )(*(pltpu.with_memory_space_constraint(x, pltpu.VMEM) for x in (new_table, new_accum, fresh)))
    return new_table, new_accum, fresh.reshape(-1, width)


def solution(mesh):
    rows, slots = P(("aa", "ba"), None), P(("aa", "ba"))
    return jax.shard_map(
        on_device,
        mesh=mesh,
        in_specs=(rows, slots, slots, slots, rows, rows),
        out_specs=(rows, rows, rows),
        check_vma=False,
    )
```

```python
import jax
import jax.numpy as jnp
from jax import lax
from jax.experimental import pallas as pl
from jax.experimental.pallas import tpu as pltpu
from jax.sharding import PartitionSpec as P

learn_rate = 0.1
epsilon = 1e-08
MESH = pl.DeviceIdType.MESH
DMA = pltpu.SemaphoreType.DMA


def offset(p):
    return (p + 1) // 2 * (2 * (p % 2) - 1)


def partner(b, k):
    core, y, x = b % 2, b // 2 % 4, b // 8
    return ((x + k // 8) % 4 * 4 + (y + k // 2 % 4) % 4) * 2 + (core + k % 2) % 2


def partner_back(b, k):
    core, y, x = b % 2, b // 2 % 4, b // 8
    return ((x + 4 - k // 8) % 4 * 4 + (y + 4 - k // 2 % 4) % 4) * 2 + (core + k % 2) % 2


def landed(ref, sem):
    pltpu.make_async_copy(ref, ref, sem).wait()


def send(src, dst, send_sem, recv_sem, a, b):
    pltpu.make_async_remote_copy(
        src, dst, send_sem, recv_sem, device_id=(a, b), device_id_type=MESH
    ).start()


def swap_blocks(m):
    row = lax.broadcasted_iota(jnp.int32, m.shape, 0)
    block = lax.broadcasted_iota(jnp.int32, m.shape, 1) // 16
    out = jnp.zeros_like(m)
    for d in range(8):
        t = m if d == 0 else pltpu.roll(pltpu.roll(m, 8 - d, 0), 16 * d, 1)
        out = jnp.where(block == (row + d) % 8, t, out)
    return out


def kernel(
    deltas, ids, counts, live, table, accum,
    tab, acc, fresh,
    src, numer, inverse, totals, first, upper, got, rep, ints, id_src, id_mid, id_row, id_got, lows,
    in_sem, tab_sem, acc_sem, int_sem, own_sem, ready,
    id_zsend, id_zrecv, id_bsend, id_brecv, dsend, drecv, rsend, rrecv,
):
    a, b = lax.axis_index("aa"), lax.axis_index("ba")
    me = 32 * a + b
    rows = tab.shape[0]
    load_ints = [
        pltpu.make_async_copy(x, ints.at[i], int_sem.at[i]) for i, x in enumerate((ids, counts, live))
    ]
    load_src = pltpu.make_async_copy(deltas, src, in_sem)
    load_tab = pltpu.make_async_copy(table, tab, tab_sem)
    load_acc = pltpu.make_async_copy(accum, acc, acc_sem)
    for copy in (*load_ints, load_src, load_tab, load_acc):
        copy.start()

    barrier = pltpu.get_barrier_semaphore()
    for d in range(1, 8):
        pl.semaphore_signal(barrier, inc=1, device_id=((a + d) % 8, b), device_id_type=MESH)

    for k in range(1, 32):
        pl.semaphore_signal(barrier, inc=1, device_id=(a, partner(b, k)), device_id_type=MESH)
    for copy in load_ints:
        copy.wait()
    packed = ints[0] + ints[1] * ints[2] * 65536
    for i in range(8):
        id_src[i] = packed[4 * i : 4 * i + 4]
    load_src.wait()
    pl.semaphore_wait(barrier, 38)
    for d in range(1, 8):
        pl.semaphore_signal(ready, inc=1, device_id=((a + d) % 8, b), device_id_type=MESH)

    def ids_along(p, _):
        pa = (a + offset(p) + 8) % 8
        send(id_src.at[pa], id_mid.at[p], id_zsend, id_zrecv, pa, b)
        return 0

    lax.fori_loop(1, 8, ids_along, 0)
    id_mid[0] = id_src[a]

    def deltas_to(k, p):
        group = k // 4 + k // 30
        pa, pb = (a + offset(p) + 8) % 8, partner(b, k)
        send(src.at[32 * pa + pb], got.at[8 * k + p], dsend, drecv.at[group], pa, pb)

    def plane_near(p, _):
        deltas_to(0, p)
        return 0

    own = pltpu.make_async_copy(src.at[me], got.at[0], own_sem)
    own.start()
    lax.fori_loop(1, 8, plane_near, 0)
    pl.semaphore_wait(ready, 7)

    def plane(k, _):
        for p in (7, 5, 6, 3, 4, 1, 2, 0):
            deltas_to(k, p)
        return 0

    lax.fori_loop(1, 10, plane, 0)
    landed(id_mid.at[pl.ds(1, 7)], id_zrecv)
    for r in range(4):
        id_row[8 * r : 8 * r + 8, 0, :] = swap_blocks(id_mid[:, r, :])

    def ids_across(k, _):
        pb = partner(b, k)
        send(id_row.at[pb], id_got.at[k], id_bsend, id_brecv, a, pb)
        return 0

    lax.fori_loop(1, 32, ids_across, 0)
    id_got[0] = id_row[b]
    lax.fori_loop(10, 32, plane, 0)
    numer[...] = jnp.zeros_like(numer)
    totals[...] = jnp.zeros_like(totals)
    landed(id_got.at[pl.ds(0, 31)], id_brecv)

    def weights(k, n):
        width = 128 * n
        both = jnp.concatenate([id_got[k + i] for i in range(n)], axis=1)
        row = both % 65536
        weight = (both // 65536).astype(jnp.float32)
        low = lax.broadcasted_iota(jnp.int32, (256, width), 0) == row % 256
        lows[:, 0:width] = jnp.where(low, 1.0, 0.0).astype(jnp.bfloat16)
        return row // 256, weight

    def add_totals(g, _):
        high, weight = weights(4 * g, 4)
        here = lax.broadcasted_iota(jnp.int32, (rows // 256, 512), 0) == high
        totals[...] += lax.dot_general(
            jnp.where(here, weight, 0.0).astype(jnp.bfloat16),
            lows[...],
            (((1,), (1,)), ((), ())),
            preferred_element_type=jnp.float32,
        )
        return 0

    def partial(high, weight, values, i, step):
        width = values.shape[0]
        picks = []
        for j in range(step // 256):
            w = jnp.where(high == i * (step // 256) + j, weight, 0.0)
            w = jnp.broadcast_to(w, (16, width)).astype(jnp.bfloat16)
            picks.append(lows[:, 0:width] * jnp.concatenate([w] * 16, axis=0))
        return jnp.dot(jnp.concatenate(picks, axis=0), values, preferred_element_type=jnp.float32)

    def arrived(k, n, count, group):
        landed(got.at[pl.ds(0, count)], drecv.at[group])
        return got[pl.ds(8 * k, 8 * n)].reshape(128 * n, 128)

    def scatter(k, n, count, group):
        high, weight = weights(k, n)
        values = arrived(k, n, count, group)

        def block(i, _):
            at = pl.ds(pl.multiple_of(i * STEP, STEP), STEP)
            numer[at, :] += partial(high, weight, values, i, STEP)
            return 0

        lax.fori_loop(0, rows // STEP, block, 0)

    def one_hot(k, n):
        columns = [jnp.broadcast_to(id_got[k + i] % 65536, (128, 128)).T for i in range(n)]
        row = jnp.concatenate(columns, axis=0)
        high = (row // 256).astype(jnp.float32).astype(jnp.bfloat16)
        lane = lax.broadcasted_iota(jnp.int32, row.shape, 1)
        row = row % 256
        near = jnp.where(row == lane, 1.0, 0.0).astype(jnp.bfloat16)
        far = jnp.where(row == lane + 128, 1.0, 0.0).astype(jnp.bfloat16)
        low = jnp.concatenate([near, far], axis=1)
        high = jnp.concatenate([high, high], axis=1)
        zero = jnp.zeros_like(low)
        return jnp.concatenate(
            [jnp.where(high == float(k), low, zero) for k in range(rows // 256)], axis=1
        )

    lax.fori_loop(0, 8, add_totals, 0)
    inv = 1.0 / jnp.maximum(totals[...], 1.0)
    for h in range(rows // 256):
        inverse[256 * h : 256 * h + 256, :] = jnp.broadcast_to(inv[h : h + 1, :], (128, 256)).T
    first[...] = one_hot(0, 1)

    own.wait()
    scatter(0, 4, 31, 0)

    def incoming(g, _):
        scatter(4 * g, 4, 32, g)
        return 0

    lax.fori_loop(1, 7, incoming, 0)
    scatter(28, 2, 16, 7)

    high, weight = weights(30, 2)
    load_tab.wait()
    load_acc.wait()
    values = arrived(30, 2, 16, 8)

    def update(i, _):
        at = pl.ds(pl.multiple_of(i * USTEP, USTEP), USTEP)
        grad = (numer[at, :] + partial(high, weight, values, i, USTEP)) * inverse[at, :]
        accum_next = acc[at, :] + grad * grad
        table_next = tab[at, :] - learn_rate * grad / (jnp.sqrt(accum_next) + epsilon)
        acc[at, :] = accum_next
        tab[at, :] = table_next
        upper[at, :] = table_next.astype(jnp.bfloat16)
        return 0

    lax.fori_loop(0, rows // USTEP, update, 0)

    def gather(k, n, picks):
        total = jnp.dot(picks, upper[...], preferred_element_type=jnp.float32)
        rep[pl.ds(8 * k, 8 * n)] = total.astype(jnp.bfloat16).reshape(8 * n, 16, 128)

    def reply(k, p):
        pa, pb = (a - offset(p) + 8) % 8, partner_back(b, k)
        send(rep.at[8 * k + p], fresh.at[me], rsend, rrecv, pa, pb)

    def replies(k, _):
        for p in (7, 5, 6, 3, 4, 1, 2, 0):
            reply(k, p)
        return 0

    gather(0, 1, first[...])
    for p in range(7, 0, -1):
        reply(0, p)
    back = pltpu.make_async_copy(rep.at[0], fresh.at[me], own_sem)
    back.start()
    gather(1, 3, one_hot(1, 3))
    lax.fori_loop(1, 4, replies, 0)

    def outgoing(g, _):
        gather(4 * g, 4, one_hot(4 * g, 4))
        lax.fori_loop(4 * g, 4 * g + 4, replies, 0)
        return 0

    lax.fori_loop(1, 8, outgoing, 0)

    landed(id_src.at[pl.ds(0, 7)], id_zsend)
    landed(id_row.at[pl.ds(0, 31)], id_bsend)
    back.wait()
    landed(got.at[pl.ds(0, 255)], dsend)
    landed(rep.at[pl.ds(0, 255)], rsend)
    landed(fresh.at[pl.ds(0, 255)], rrecv)


STEP = 2048
USTEP = 2048
LIMIT = 46


def write_out(a, b, c, a_out, b_out, c_out, *sems):
    copies = [
        pltpu.make_async_copy(x, y, sem) for x, y, sem in zip((a, b, c), (a_out, b_out, c_out), sems)
    ]
    for copy in copies:
        copy.start()
    for copy in copies:
        copy.wait()


def on_device(deltas, row_ids, sample_counts, live, table, accum):
    rows, width = table.shape
    blocks = (256, 16, width)
    small = (32, 128)
    vmem = pl.BlockSpec(memory_space=pltpu.VMEM)
    hbm = pl.BlockSpec(memory_space=pltpu.HBM)
    bf16, f32, i32 = jnp.bfloat16, jnp.float32, jnp.int32
    V = pltpu.VMEM
    new_table, new_accum, fresh = pl.pallas_call(
        kernel,
        name="exchange",
        out_shape=(
            jax.ShapeDtypeStruct((rows, width), f32),
            jax.ShapeDtypeStruct((rows, width), f32),
            jax.ShapeDtypeStruct(blocks, bf16),
        ),
        in_specs=[hbm] * 6,
        out_specs=(vmem, vmem, vmem),
        scratch_shapes=[
            V(blocks, bf16), V((rows, width), f32), V((rows, width), f32),
            V((rows // 256, 256), f32), V((width, rows), bf16),
            V((rows, width), bf16), V(blocks, bf16), V(blocks, bf16), V((3, 32, 128), i32),
            V((8, 4, 128), i32), V((8, 4, 128), i32), V((32, 1, 128), i32), V((32, 1, 128), i32),
            V((256, 512), bf16),
            DMA, DMA, DMA, DMA((3,)), DMA, pltpu.SemaphoreType.REGULAR,
            DMA, DMA, DMA, DMA, DMA, DMA((9,)), DMA, DMA,
        ],
        compiler_params=pltpu.CompilerParams(
            collective_id=1, has_side_effects=True, vmem_limit_bytes=LIMIT << 20
        ),
    )(
        *(pltpu.with_memory_space_constraint(x, pltpu.HBM) for x in (
        deltas.reshape(blocks), row_ids.reshape(small), sample_counts.reshape(small),
        live.reshape(small), table, accum)),
    )
    new_table, new_accum, fresh = pl.pallas_call(
        write_out,
        name="write_out",
        out_shape=(
            jax.ShapeDtypeStruct((rows, width), f32),
            jax.ShapeDtypeStruct((rows, width), f32),
            jax.ShapeDtypeStruct(blocks, bf16),
        ),
        in_specs=[vmem] * 3,
        out_specs=(hbm, hbm, hbm),
        scratch_shapes=[DMA, DMA, DMA],
        compiler_params=pltpu.CompilerParams(vmem_limit_bytes=2 << 20),
    )(*(pltpu.with_memory_space_constraint(x, pltpu.VMEM) for x in (new_table, new_accum, fresh)))
    return new_table, new_accum, fresh.reshape(-1, width)


def solution(mesh):
    rows, slots = P(("aa", "ba"), None), P(("aa", "ba"))
    return jax.shard_map(
        on_device,
        mesh=mesh,
        in_specs=(rows, slots, slots, slots, rows, rows),
        out_specs=(rows, rows, rows),
        check_vma=False,
    )
```

```python
import jax
import jax.numpy as jnp
from jax import lax
from jax.experimental import pallas as pl
from jax.experimental.pallas import tpu as pltpu
from jax.sharding import PartitionSpec as P

learn_rate = 0.1
epsilon = 1e-08
MESH = pl.DeviceIdType.MESH
DMA = pltpu.SemaphoreType.DMA


def offset(p):
    return (p + 1) // 2 * (2 * (p % 2) - 1)


def partner(b, k):
    core, y, x = b % 2, b // 2 % 4, b // 8
    return ((x + k // 8) % 4 * 4 + (y + k // 2 % 4) % 4) * 2 + (core + k % 2) % 2


def partner_back(b, k):
    core, y, x = b % 2, b // 2 % 4, b // 8
    return ((x + 4 - k // 8) % 4 * 4 + (y + 4 - k // 2 % 4) % 4) * 2 + (core + k % 2) % 2


def landed(ref, sem):
    pltpu.make_async_copy(ref, ref, sem).wait()


def send(src, dst, send_sem, recv_sem, a, b):
    pltpu.make_async_remote_copy(
        src, dst, send_sem, recv_sem, device_id=(a, b), device_id_type=MESH
    ).start()


def swap_blocks(m):
    row = lax.broadcasted_iota(jnp.int32, m.shape, 0)
    block = lax.broadcasted_iota(jnp.int32, m.shape, 1) // 16
    out = jnp.zeros_like(m)
    for d in range(8):
        t = m if d == 0 else pltpu.roll(pltpu.roll(m, 8 - d, 0), 16 * d, 1)
        out = jnp.where(block == (row + d) % 8, t, out)
    return out


def kernel(
    deltas, ids, counts, live, table, accum,
    tab, acc, fresh,
    src, numer, inverse, totals, first, upper, got, rep, ints, id_src, id_mid, id_row, id_got, lows,
    in_sem, tab_sem, acc_sem, int_sem, own_sem, ready,
    id_zsend, id_zrecv, id_bsend, id_brecv, dsend, drecv, rsend, rrecv,
):
    a, b = lax.axis_index("aa"), lax.axis_index("ba")
    me = 32 * a + b
    rows = tab.shape[0]
    load_ints = [
        pltpu.make_async_copy(x, ints.at[i], int_sem.at[i]) for i, x in enumerate((ids, counts, live))
    ]
    load_src = pltpu.make_async_copy(deltas, src, in_sem)
    load_tab = pltpu.make_async_copy(table, tab, tab_sem)
    load_acc = pltpu.make_async_copy(accum, acc, acc_sem)
    for copy in (*load_ints, load_src, load_tab, load_acc):
        copy.start()

    barrier = pltpu.get_barrier_semaphore()
    for d in range(1, 8):
        pl.semaphore_signal(barrier, inc=1, device_id=((a + d) % 8, b), device_id_type=MESH)

    for k in range(1, 32):
        pl.semaphore_signal(barrier, inc=1, device_id=(a, partner(b, k)), device_id_type=MESH)
    for copy in load_ints:
        copy.wait()
    packed = ints[0] + ints[1] * ints[2] * 65536
    for i in range(8):
        id_src[i] = packed[4 * i : 4 * i + 4]
    load_src.wait()
    pl.semaphore_wait(barrier, 38)
    for d in range(1, 8):
        pl.semaphore_signal(ready, inc=1, device_id=((a + d) % 8, b), device_id_type=MESH)

    def ids_along(p, _):
        pa = (a + offset(p) + 8) % 8
        send(id_src.at[pa], id_mid.at[p], id_zsend, id_zrecv, pa, b)
        return 0

    lax.fori_loop(1, 8, ids_along, 0)
    id_mid[0] = id_src[a]

    def deltas_to(k, p):
        group = k // 4 + k // 30
        pa, pb = (a + offset(p) + 8) % 8, partner(b, k)
        send(src.at[32 * pa + pb], got.at[8 * k + p], dsend, drecv.at[group], pa, pb)

    def plane_near(p, _):
        deltas_to(0, p)
        return 0

    own = pltpu.make_async_copy(src.at[me], got.at[0], own_sem)
    own.start()
    lax.fori_loop(1, 8, plane_near, 0)

    def plane_far(k, _):
        deltas_to(k, 0)
        return 0

    lax.fori_loop(1, 32, plane_far, 0)
    pl.semaphore_wait(ready, 7)

    def plane(k, _):
        for p in (7, 5, 6, 3, 4, 1, 2):
            deltas_to(k, p)
        return 0

    lax.fori_loop(1, 10, plane, 0)
    landed(id_mid.at[pl.ds(1, 7)], id_zrecv)
    for r in range(4):
        id_row[8 * r : 8 * r + 8, 0, :] = swap_blocks(id_mid[:, r, :])

    def ids_across(k, _):
        pb = partner(b, k)
        send(id_row.at[pb], id_got.at[k], id_bsend, id_brecv, a, pb)
        return 0

    lax.fori_loop(1, 32, ids_across, 0)
    id_got[0] = id_row[b]
    lax.fori_loop(10, 32, plane, 0)
    numer[...] = jnp.zeros_like(numer)
    totals[...] = jnp.zeros_like(totals)
    landed(id_got.at[pl.ds(0, 31)], id_brecv)

    def weights(k, n):
        width = 128 * n
        both = jnp.concatenate([id_got[k + i] for i in range(n)], axis=1)
        row = both % 65536
        weight = (both // 65536).astype(jnp.float32)
        low = lax.broadcasted_iota(jnp.int32, (256, width), 0) == row % 256
        lows[:, 0:width] = jnp.where(low, 1.0, 0.0).astype(jnp.bfloat16)
        return row // 256, weight

    def add_totals(g, _):
        high, weight = weights(4 * g, 4)
        here = lax.broadcasted_iota(jnp.int32, (rows // 256, 512), 0) == high
        totals[...] += lax.dot_general(
            jnp.where(here, weight, 0.0).astype(jnp.bfloat16),
            lows[...],
            (((1,), (1,)), ((), ())),
            preferred_element_type=jnp.float32,
        )
        return 0

    def partial(high, weight, values, i, step):
        width = values.shape[0]
        picks = []
        for j in range(step // 256):
            w = jnp.where(high == i * (step // 256) + j, weight, 0.0)
            w = jnp.broadcast_to(w, (16, width)).astype(jnp.bfloat16)
            picks.append(lows[:, 0:width] * jnp.concatenate([w] * 16, axis=0))
        return jnp.dot(jnp.concatenate(picks, axis=0), values, preferred_element_type=jnp.float32)

    def arrived(k, n, count, group):
        landed(got.at[pl.ds(0, count)], drecv.at[group])
        return got[pl.ds(8 * k, 8 * n)].reshape(128 * n, 128)

    def scatter(k, n, count, group):
        high, weight = weights(k, n)
        values = arrived(k, n, count, group)

        def block(i, _):
            at = pl.ds(pl.multiple_of(i * STEP, STEP), STEP)
            numer[at, :] += partial(high, weight, values, i, STEP)
            return 0

        lax.fori_loop(0, rows // STEP, block, 0)

    def one_hot(k, n):
        columns = [jnp.broadcast_to(id_got[k + i] % 65536, (128, 128)).T for i in range(n)]
        row = jnp.concatenate(columns, axis=0)
        high = (row // 256).astype(jnp.float32).astype(jnp.bfloat16)
        lane = lax.broadcasted_iota(jnp.int32, row.shape, 1)
        row = row % 256
        near = jnp.where(row == lane, 1.0, 0.0).astype(jnp.bfloat16)
        far = jnp.where(row == lane + 128, 1.0, 0.0).astype(jnp.bfloat16)
        low = jnp.concatenate([near, far], axis=1)
        high = jnp.concatenate([high, high], axis=1)
        zero = jnp.zeros_like(low)
        return jnp.concatenate(
            [jnp.where(high == float(k), low, zero) for k in range(rows // 256)], axis=1
        )

    lax.fori_loop(0, 8, add_totals, 0)
    inv = 1.0 / jnp.maximum(totals[...], 1.0)
    for h in range(rows // 256):
        inverse[256 * h : 256 * h + 256, :] = jnp.broadcast_to(inv[h : h + 1, :], (128, 256)).T
    first[...] = one_hot(0, 1)

    own.wait()
    scatter(0, 4, 31, 0)

    def incoming(g, _):
        scatter(4 * g, 4, 32, g)
        return 0

    lax.fori_loop(1, 7, incoming, 0)
    scatter(28, 2, 16, 7)

    high, weight = weights(30, 2)
    load_tab.wait()
    load_acc.wait()
    values = arrived(30, 2, 16, 8)

    def update(i, _):
        at = pl.ds(pl.multiple_of(i * USTEP, USTEP), USTEP)
        grad = (numer[at, :] + partial(high, weight, values, i, USTEP)) * inverse[at, :]
        accum_next = acc[at, :] + grad * grad
        table_next = tab[at, :] - learn_rate * grad / (jnp.sqrt(accum_next) + epsilon)
        acc[at, :] = accum_next
        tab[at, :] = table_next
        upper[at, :] = table_next.astype(jnp.bfloat16)
        return 0

    lax.fori_loop(0, rows // USTEP, update, 0)

    def gather(k, n, picks):
        total = jnp.dot(picks, upper[...], preferred_element_type=jnp.float32)
        rep[pl.ds(8 * k, 8 * n)] = total.astype(jnp.bfloat16).reshape(8 * n, 16, 128)

    def reply(k, p):
        pa, pb = (a - offset(p) + 8) % 8, partner_back(b, k)
        send(rep.at[8 * k + p], fresh.at[me], rsend, rrecv, pa, pb)

    def replies(k, _):
        for p in (7, 5, 6, 3, 4, 1, 2, 0):
            reply(k, p)
        return 0

    gather(0, 1, first[...])
    for p in range(7, 0, -1):
        reply(0, p)
    back = pltpu.make_async_copy(rep.at[0], fresh.at[me], own_sem)
    back.start()
    gather(1, 3, one_hot(1, 3))
    lax.fori_loop(1, 4, replies, 0)

    def outgoing(g, _):
        gather(4 * g, 4, one_hot(4 * g, 4))
        lax.fori_loop(4 * g, 4 * g + 4, replies, 0)
        return 0

    lax.fori_loop(1, 8, outgoing, 0)

    landed(id_src.at[pl.ds(0, 7)], id_zsend)
    landed(id_row.at[pl.ds(0, 31)], id_bsend)
    back.wait()
    landed(got.at[pl.ds(0, 255)], dsend)
    landed(rep.at[pl.ds(0, 255)], rsend)
    landed(fresh.at[pl.ds(0, 255)], rrecv)


STEP = 2048
USTEP = 2048
LIMIT = 46


def write_out(a, b, c, a_out, b_out, c_out, *sems):
    copies = [
        pltpu.make_async_copy(x, y, sem) for x, y, sem in zip((a, b, c), (a_out, b_out, c_out), sems)
    ]
    for copy in copies:
        copy.start()
    for copy in copies:
        copy.wait()


def on_device(deltas, row_ids, sample_counts, live, table, accum):
    rows, width = table.shape
    blocks = (256, 16, width)
    small = (32, 128)
    vmem = pl.BlockSpec(memory_space=pltpu.VMEM)
    hbm = pl.BlockSpec(memory_space=pltpu.HBM)
    bf16, f32, i32 = jnp.bfloat16, jnp.float32, jnp.int32
    V = pltpu.VMEM
    new_table, new_accum, fresh = pl.pallas_call(
        kernel,
        name="exchange",
        out_shape=(
            jax.ShapeDtypeStruct((rows, width), f32),
            jax.ShapeDtypeStruct((rows, width), f32),
            jax.ShapeDtypeStruct(blocks, bf16),
        ),
        in_specs=[hbm] * 6,
        out_specs=(vmem, vmem, vmem),
        scratch_shapes=[
            V(blocks, bf16), V((rows, width), f32), V((rows, width), f32),
            V((rows // 256, 256), f32), V((width, rows), bf16),
            V((rows, width), bf16), V(blocks, bf16), V(blocks, bf16), V((3, 32, 128), i32),
            V((8, 4, 128), i32), V((8, 4, 128), i32), V((32, 1, 128), i32), V((32, 1, 128), i32),
            V((256, 512), bf16),
            DMA, DMA, DMA, DMA((3,)), DMA, pltpu.SemaphoreType.REGULAR,
            DMA, DMA, DMA, DMA, DMA, DMA((9,)), DMA, DMA,
        ],
        compiler_params=pltpu.CompilerParams(
            collective_id=1, has_side_effects=True, vmem_limit_bytes=LIMIT << 20
        ),
    )(
        *(pltpu.with_memory_space_constraint(x, pltpu.HBM) for x in (
        deltas.reshape(blocks), row_ids.reshape(small), sample_counts.reshape(small),
        live.reshape(small), table, accum)),
    )
    new_table, new_accum, fresh = pl.pallas_call(
        write_out,
        name="write_out",
        out_shape=(
            jax.ShapeDtypeStruct((rows, width), f32),
            jax.ShapeDtypeStruct((rows, width), f32),
            jax.ShapeDtypeStruct(blocks, bf16),
        ),
        in_specs=[vmem] * 3,
        out_specs=(hbm, hbm, hbm),
        scratch_shapes=[DMA, DMA, DMA],
        compiler_params=pltpu.CompilerParams(vmem_limit_bytes=2 << 20),
    )(*(pltpu.with_memory_space_constraint(x, pltpu.VMEM) for x in (new_table, new_accum, fresh)))
    return new_table, new_accum, fresh.reshape(-1, width)


def solution(mesh):
    rows, slots = P(("aa", "ba"), None), P(("aa", "ba"))
    return jax.shard_map(
        on_device,
        mesh=mesh,
        in_specs=(rows, slots, slots, slots, rows, rows),
        out_specs=(rows, rows, rows),
        check_vma=False,
    )
```

```python
import jax
import jax.numpy as jnp
from jax import lax
from jax.experimental import pallas as pl
from jax.experimental.pallas import tpu as pltpu
from jax.sharding import PartitionSpec as P

learn_rate = 0.1
epsilon = 1e-08
MESH = pl.DeviceIdType.MESH
DMA = pltpu.SemaphoreType.DMA


def offset(p):
    return (p + 1) // 2 * (2 * (p % 2) - 1)


def partner(b, k):
    core, y, x = b % 2, b // 2 % 4, b // 8
    return ((x + k // 8) % 4 * 4 + (y + k // 2 % 4) % 4) * 2 + (core + k % 2) % 2


def partner_back(b, k):
    core, y, x = b % 2, b // 2 % 4, b // 8
    return ((x + 4 - k // 8) % 4 * 4 + (y + 4 - k // 2 % 4) % 4) * 2 + (core + k % 2) % 2


def landed(ref, sem):
    pltpu.make_async_copy(ref, ref, sem).wait()


def send(src, dst, send_sem, recv_sem, a, b):
    pltpu.make_async_remote_copy(
        src, dst, send_sem, recv_sem, device_id=(a, b), device_id_type=MESH
    ).start()


def swap_blocks(m):
    row = lax.broadcasted_iota(jnp.int32, m.shape, 0)
    block = lax.broadcasted_iota(jnp.int32, m.shape, 1) // 16
    out = jnp.zeros_like(m)
    for d in range(8):
        t = m if d == 0 else pltpu.roll(pltpu.roll(m, 8 - d, 0), 16 * d, 1)
        out = jnp.where(block == (row + d) % 8, t, out)
    return out


def kernel(
    deltas, ids, counts, live, table, accum,
    tab, acc, fresh,
    src, numer, inverse, totals, first, second, upper, got, rep, ints, id_src, id_mid, id_row, id_got, lows,
    in_sem, tab_sem, acc_sem, int_sem, own_sem, ready,
    id_zsend, id_zrecv, id_bsend, id_brecv, dsend, drecv, rsend, rrecv,
):
    a, b = lax.axis_index("aa"), lax.axis_index("ba")
    me = 32 * a + b
    rows = tab.shape[0]
    load_ints = [
        pltpu.make_async_copy(x, ints.at[i], int_sem.at[i]) for i, x in enumerate((ids, counts, live))
    ]
    load_src = pltpu.make_async_copy(deltas, src, in_sem)
    load_tab = pltpu.make_async_copy(table, tab, tab_sem)
    load_acc = pltpu.make_async_copy(accum, acc, acc_sem)
    for copy in (*load_ints, load_src, load_tab, load_acc):
        copy.start()

    barrier = pltpu.get_barrier_semaphore()
    for d in range(1, 8):
        pl.semaphore_signal(barrier, inc=1, device_id=((a + d) % 8, b), device_id_type=MESH)

    for k in range(1, 32):
        pl.semaphore_signal(barrier, inc=1, device_id=(a, partner(b, k)), device_id_type=MESH)
    for copy in load_ints:
        copy.wait()
    packed = ints[0] + ints[1] * ints[2] * 65536
    for i in range(8):
        id_src[i] = packed[4 * i : 4 * i + 4]
    load_src.wait()
    pl.semaphore_wait(barrier, 38)
    for d in range(1, 8):
        pl.semaphore_signal(ready, inc=1, device_id=((a + d) % 8, b), device_id_type=MESH)

    def ids_along(p, _):
        pa = (a + offset(p) + 8) % 8
        send(id_src.at[pa], id_mid.at[p], id_zsend, id_zrecv, pa, b)
        return 0

    lax.fori_loop(1, 8, ids_along, 0)
    id_mid[0] = id_src[a]

    def deltas_to(k, p):
        group = k // 4 + k // 30
        pa, pb = (a + offset(p) + 8) % 8, partner(b, k)
        send(src.at[32 * pa + pb], got.at[8 * k + p], dsend, drecv.at[group], pa, pb)

    def plane_near(p, _):
        deltas_to(0, p)
        return 0

    own = pltpu.make_async_copy(src.at[me], got.at[0], own_sem)
    own.start()
    lax.fori_loop(1, 8, plane_near, 0)

    def plane_far(k, _):
        deltas_to(k, 0)
        return 0

    lax.fori_loop(1, 32, plane_far, 0)
    pl.semaphore_wait(ready, 7)

    def plane(k, _):
        for p in (7, 5, 6, 3, 4, 1, 2):
            deltas_to(k, p)
        return 0

    lax.fori_loop(1, 10, plane, 0)
    landed(id_mid.at[pl.ds(1, 7)], id_zrecv)
    for r in range(4):
        id_row[8 * r : 8 * r + 8, 0, :] = swap_blocks(id_mid[:, r, :])

    def ids_across(k, _):
        pb = partner(b, k)
        send(id_row.at[pb], id_got.at[k], id_bsend, id_brecv, a, pb)
        return 0

    lax.fori_loop(1, 32, ids_across, 0)
    id_got[0] = id_row[b]
    lax.fori_loop(10, 32, plane, 0)
    numer[...] = jnp.zeros_like(numer)
    totals[...] = jnp.zeros_like(totals)
    landed(id_got.at[pl.ds(0, 31)], id_brecv)

    def weights(k, n):
        width = 128 * n
        both = jnp.concatenate([id_got[k + i] for i in range(n)], axis=1)
        row = both % 65536
        weight = (both // 65536).astype(jnp.float32)
        low = lax.broadcasted_iota(jnp.int32, (256, width), 0) == row % 256
        lows[:, 0:width] = jnp.where(low, 1.0, 0.0).astype(jnp.bfloat16)
        return row // 256, weight

    def add_totals(g, _):
        high, weight = weights(4 * g, 4)
        here = lax.broadcasted_iota(jnp.int32, (rows // 256, 512), 0) == high
        totals[...] += lax.dot_general(
            jnp.where(here, weight, 0.0).astype(jnp.bfloat16),
            lows[...],
            (((1,), (1,)), ((), ())),
            preferred_element_type=jnp.float32,
        )
        return 0

    def partial(high, weight, values, i, step):
        width = values.shape[0]
        picks = []
        for j in range(step // 256):
            w = jnp.where(high == i * (step // 256) + j, weight, 0.0)
            w = jnp.broadcast_to(w, (16, width)).astype(jnp.bfloat16)
            picks.append(lows[:, 0:width] * jnp.concatenate([w] * 16, axis=0))
        return jnp.dot(jnp.concatenate(picks, axis=0), values, preferred_element_type=jnp.float32)

    def arrived(k, n, count, group):
        landed(got.at[pl.ds(0, count)], drecv.at[group])
        return got[pl.ds(8 * k, 8 * n)].reshape(128 * n, 128)

    def scatter(k, n, count, group):
        high, weight = weights(k, n)
        values = arrived(k, n, count, group)

        def block(i, _):
            at = pl.ds(pl.multiple_of(i * STEP, STEP), STEP)
            numer[at, :] += partial(high, weight, values, i, STEP)
            return 0

        lax.fori_loop(0, rows // STEP, block, 0)

    def one_hot(k, n):
        columns = [jnp.broadcast_to(id_got[k + i] % 65536, (128, 128)).T for i in range(n)]
        row = jnp.concatenate(columns, axis=0)
        high = (row // 256).astype(jnp.float32).astype(jnp.bfloat16)
        lane = lax.broadcasted_iota(jnp.int32, row.shape, 1)
        row = row % 256
        near = jnp.where(row == lane, 1.0, 0.0).astype(jnp.bfloat16)
        far = jnp.where(row == lane + 128, 1.0, 0.0).astype(jnp.bfloat16)
        low = jnp.concatenate([near, far], axis=1)
        high = jnp.concatenate([high, high], axis=1)
        zero = jnp.zeros_like(low)
        return jnp.concatenate(
            [jnp.where(high == float(k), low, zero) for k in range(rows // 256)], axis=1
        )

    lax.fori_loop(0, 8, add_totals, 0)
    inv = 1.0 / jnp.maximum(totals[...], 1.0)
    for h in range(rows // 256):
        inverse[256 * h : 256 * h + 256, :] = jnp.broadcast_to(inv[h : h + 1, :], (128, 256)).T
    first[...] = one_hot(0, 1)
    second[...] = one_hot(1, 3)

    own.wait()
    scatter(0, 4, 31, 0)

    def incoming(g, _):
        scatter(4 * g, 4, 32, g)
        return 0

    lax.fori_loop(1, 7, incoming, 0)
    scatter(28, 2, 16, 7)

    high, weight = weights(30, 2)
    load_tab.wait()
    load_acc.wait()
    values = arrived(30, 2, 16, 8)

    def update(i, _):
        at = pl.ds(pl.multiple_of(i * USTEP, USTEP), USTEP)
        grad = (numer[at, :] + partial(high, weight, values, i, USTEP)) * inverse[at, :]
        accum_next = acc[at, :] + grad * grad
        table_next = tab[at, :] - learn_rate * grad / (jnp.sqrt(accum_next) + epsilon)
        acc[at, :] = accum_next
        tab[at, :] = table_next
        upper[at, :] = table_next.astype(jnp.bfloat16)
        return 0

    lax.fori_loop(0, rows // USTEP, update, 0)

    def gather(k, n, picks):
        total = jnp.dot(picks, upper[...], preferred_element_type=jnp.float32)
        rep[pl.ds(8 * k, 8 * n)] = total.astype(jnp.bfloat16).reshape(8 * n, 16, 128)

    def reply(k, p):
        pa, pb = (a - offset(p) + 8) % 8, partner_back(b, k)
        send(rep.at[8 * k + p], fresh.at[me], rsend, rrecv, pa, pb)

    def replies(k, _):
        for p in (7, 5, 6, 3, 4, 1, 2, 0):
            reply(k, p)
        return 0

    gather(0, 1, first[...])
    for p in range(7, 0, -1):
        reply(0, p)
    back = pltpu.make_async_copy(rep.at[0], fresh.at[me], own_sem)
    back.start()
    gather(1, 3, second[...])
    lax.fori_loop(1, 4, replies, 0)

    def outgoing(g, _):
        gather(4 * g, 4, one_hot(4 * g, 4))
        lax.fori_loop(4 * g, 4 * g + 4, replies, 0)
        return 0

    lax.fori_loop(1, 8, outgoing, 0)

    landed(id_src.at[pl.ds(0, 7)], id_zsend)
    landed(id_row.at[pl.ds(0, 31)], id_bsend)
    back.wait()
    landed(got.at[pl.ds(0, 255)], dsend)
    landed(rep.at[pl.ds(0, 255)], rsend)
    landed(fresh.at[pl.ds(0, 255)], rrecv)


STEP = 2048
USTEP = 2048
LIMIT = 46


def write_out(a, b, c, a_out, b_out, c_out, *sems):
    copies = [
        pltpu.make_async_copy(x, y, sem) for x, y, sem in zip((a, b, c), (a_out, b_out, c_out), sems)
    ]
    for copy in copies:
        copy.start()
    for copy in copies:
        copy.wait()


def on_device(deltas, row_ids, sample_counts, live, table, accum):
    rows, width = table.shape
    blocks = (256, 16, width)
    small = (32, 128)
    vmem = pl.BlockSpec(memory_space=pltpu.VMEM)
    hbm = pl.BlockSpec(memory_space=pltpu.HBM)
    bf16, f32, i32 = jnp.bfloat16, jnp.float32, jnp.int32
    V = pltpu.VMEM
    new_table, new_accum, fresh = pl.pallas_call(
        kernel,
        name="exchange",
        out_shape=(
            jax.ShapeDtypeStruct((rows, width), f32),
            jax.ShapeDtypeStruct((rows, width), f32),
            jax.ShapeDtypeStruct(blocks, bf16),
        ),
        in_specs=[hbm] * 6,
        out_specs=(vmem, vmem, vmem),
        scratch_shapes=[
            V(blocks, bf16), V((rows, width), f32), V((rows, width), f32),
            V((rows // 256, 256), f32), V((width, rows), bf16), V((3 * width, rows), bf16),
            V((rows, width), bf16), V(blocks, bf16), V(blocks, bf16), V((3, 32, 128), i32),
            V((8, 4, 128), i32), V((8, 4, 128), i32), V((32, 1, 128), i32), V((32, 1, 128), i32),
            V((256, 512), bf16),
            DMA, DMA, DMA, DMA((3,)), DMA, pltpu.SemaphoreType.REGULAR,
            DMA, DMA, DMA, DMA, DMA, DMA((9,)), DMA, DMA,
        ],
        compiler_params=pltpu.CompilerParams(
            collective_id=1, has_side_effects=True, vmem_limit_bytes=LIMIT << 20
        ),
    )(
        *(pltpu.with_memory_space_constraint(x, pltpu.HBM) for x in (
        deltas.reshape(blocks), row_ids.reshape(small), sample_counts.reshape(small),
        live.reshape(small), table, accum)),
    )
    new_table, new_accum, fresh = pl.pallas_call(
        write_out,
        name="write_out",
        out_shape=(
            jax.ShapeDtypeStruct((rows, width), f32),
            jax.ShapeDtypeStruct((rows, width), f32),
            jax.ShapeDtypeStruct(blocks, bf16),
        ),
        in_specs=[vmem] * 3,
        out_specs=(hbm, hbm, hbm),
        scratch_shapes=[DMA, DMA, DMA],
        compiler_params=pltpu.CompilerParams(vmem_limit_bytes=2 << 20),
    )(*(pltpu.with_memory_space_constraint(x, pltpu.VMEM) for x in (new_table, new_accum, fresh)))
    return new_table, new_accum, fresh.reshape(-1, width)


def solution(mesh):
    rows, slots = P(("aa", "ba"), None), P(("aa", "ba"))
    return jax.shard_map(
        on_device,
        mesh=mesh,
        in_specs=(rows, slots, slots, slots, rows, rows),
        out_specs=(rows, rows, rows),
        check_vma=False,
    )
```
